32 devices in a mesh: groups: 2 (over x), seq: 16 (over z, y, core).
Axes of the slice: x: 2, y: 2, z: 4, core: 2. Of those that a mesh axis runs over, the one named last changes fastest.
Arguments:
- layer_in: bfloat16 [8192, 2560], P(('groups', 'seq')), parts along dimension 0, may hold values from -6 to 6
- ssm_in: bfloat16 [8192, 2560], P(('groups', 'seq')), parts along dimension 0, may hold values from -6 to 6
- weight_bc: bfloat16 [2560, 256], replicated, may hold values from -0.015625 to 0.015625
- weight_dt: bfloat16 [2560, 40], replicated, may hold values from -0.125 to 0.125
- bias_dt: float32 [40], replicated, may hold values from -3 to 0.5
- log_rate: float32 [40], replicated, may hold values from -13.2 to -2.9
- skip_gain: float32 [40], replicated, may hold values from 0.5 to 1.5
- grad_out: bfloat16 [8192, 2560], P(('groups', 'seq')), parts along dimension 0, may hold values from -8 to 8
Outputs:
- grad_ssm_in: bfloat16 [8192, 2560], P(('groups', 'seq')), parts along dimension 0
- grad_layer_in: bfloat16 [8192, 2560], P(('groups', 'seq')), parts along dimension 0
- grad_weight_bc: float32 [5120, 256], P(('groups', 'seq')), parts along dimension 0
- grad_weight_dt: float32 [5120, 40], P(('groups', 'seq')), parts along dimension 0
- grad_bias_dt: float32 [80], P('groups'), parts along dimension 0
- grad_log_rate: float32 [80], P('groups'), parts along dimension 0
- grad_skip_gain: float32 [80], P('groups'), parts along dimension 0
The draws below stay inside these ranges and needn't reach their ends.
There are 2 independent parts, one for each index of `groups`. The reference program is written for one: setup_inputs(seed, part) draws one part's arguments, and reference() takes and returns one part's arrays. A program takes and returns all parts, laid end to end along the dimension named above; an argument that names none is the same for every part. Nothing has to cross between parts.
All inputs are finite; a program needn't handle non-finite values.
Results may differ from the reference program's by a relative error of at most 0.0059.
Values sent between devices are 32-bit elements; how exact they have to be, the bound alone decides.
A program may use at most 128 MiB of HBM per device.

```python
import math
import jax
import jax.numpy as jnp
from jax import lax

D = 2560
HEADS = 40
HEAD_DIM = 64
STATE = 128
BLOCK = 256
LEN = 4096


def draw_log_rate(key, part):
    lowest = math.log(2e-06)
    highest = math.log(0.05)
    return jax.random.uniform(key, (HEADS,), jnp.float32, lowest, highest)


def draw_grad_out(key, part):
    shape = (LEN, HEADS * HEAD_DIM)
    position = jnp.arange(LEN, dtype=jnp.float32)[:, None] / LEN
    base = jnp.clip(jax.random.normal(key, shape, jnp.float32), -5.0, 5.0)
    result = base * (0.5 + position)
    return result.astype(jnp.bfloat16)


def block_levels(stream_key, extent, shards, least, largest):
    level, own = 1.0, jax.random.fold_in(stream_key, 6)
    for dim, blocks in shards:
        heights = jnp.exp(jax.random.uniform(jax.random.fold_in(own, dim), (blocks,), jnp.float32, least / len(shards), largest / len(shards)))
        level = level * jnp.repeat(heights, extent[dim] // blocks).reshape([-1 if axis == dim else 1 for axis in range(len(extent))])
    return level


def noise(stream_key, dims, scale, reach, cuts=(), kind=jnp.bfloat16):
    entries = jax.random.normal(stream_key, dims, jnp.float32) * scale
    if len(cuts) > 0:
        entries = block_levels(stream_key, dims, cuts, -0.22, 0.18) * entries
    return jnp.clip(entries, min=-reach, max=reach).astype(kind)


def setup_inputs(seed: int = 0, part: int = 0) -> dict:
    arg_keys = jax.random.split(jax.random.key(seed), 9)
    part_keys = jax.random.split(jax.random.fold_in(arg_keys[8], part), 9)
    return {
        "layer_in": noise(part_keys[0], (LEN, D), 1.0, 6.0, ((0, 16),)),
        "ssm_in": noise(part_keys[1], (LEN, HEADS * HEAD_DIM), 1.0, 6.0, ((0, 16),)),
        "weight_bc": noise(arg_keys[2], (D, 2 * STATE), (64 * D) ** -0.5, 0.015625),
        "weight_dt": noise(arg_keys[3], (D, HEADS), D ** -0.5, 0.125),
        "bias_dt": jnp.clip(jax.random.uniform(arg_keys[4], (HEADS,), jnp.float32, -3.0, 0.5), -3.0, 0.5),
        "log_rate": draw_log_rate(jax.random.fold_in(arg_keys[8], 71), part),
        "skip_gain": jnp.clip(jax.random.uniform(arg_keys[6], (HEADS,), jnp.float32, 0.5, 1.5), 0.5, 1.5),
        "grad_out": draw_grad_out(jax.random.fold_in(jax.random.fold_in(arg_keys[8], part), 71), part),
    }


HIGHEST = lax.Precision.HIGHEST

def block_pass(state, pieces):
    values, b_rows, c_rows, scores, step_size, log_decay = pieces
    running = jnp.cumsum(log_decay, axis=0)
    count = values.shape[0]
    indices = jnp.arange(count)
    lower_mask = indices[:, None] >= indices[None, :]
    run_heads = running.T
    spread = jnp.where(lower_mask[None, :, :], run_heads[:, :, None] - run_heads[:, None, :], -jnp.inf)
    mixing = jnp.exp(spread) * scores[None, :, :] * step_size.T[:, None, :]
    inner = jnp.einsum('hts,shp->thp', mixing, values, precision=HIGHEST)
    carried = jnp.exp(running)[:, :, None] * jnp.einsum('tn,hpn->thp', c_rows, state, precision=HIGHEST)
    tail_weight = jnp.exp(running[-1][None, :] - running) * step_size
    fresh = jnp.einsum('shp,sn->hpn', tail_weight[:, :, None] * values, b_rows, precision=HIGHEST)
    new_state = jnp.exp(running[-1])[:, None, None] * state + fresh
    return (new_state, inner + carried)

def mixer(values, b_rows, c_rows, scores, step_raw, log_rate, skip_gain):
    step_size = jax.nn.softplus(step_raw)
    log_decay = -jnp.exp(log_rate)[None, :] * step_size
    blocks = values.shape[0] // BLOCK

    def split(array):
        return array.reshape((blocks, BLOCK) + array.shape[1:])
    start = jnp.zeros((values.shape[1], values.shape[2], b_rows.shape[1]), values.dtype)
    final, outputs = lax.scan(jax.checkpoint(block_pass), start, (split(values), split(b_rows), split(c_rows), scores, split(step_size), split(log_decay)))
    return outputs.reshape(values.shape) + skip_gain[None, :, None] * values

def reference(layer_in, ssm_in, weight_bc, weight_dt, bias_dt, log_rate, skip_gain, grad_out):
    length = layer_in.shape[0]
    blocks = length // BLOCK
    proj_bc = jnp.dot(layer_in, weight_bc, preferred_element_type=jnp.float32).astype(jnp.bfloat16)
    proj_kept = lax.optimization_barrier(proj_bc)
    proj_wide = proj_kept.astype(jnp.float32)
    b_rows = proj_wide[:, :STATE]
    c_rows = proj_wide[:, STATE:]
    b_narrow = proj_kept[:, :STATE].reshape(blocks, BLOCK, STATE)
    c_narrow = proj_kept[:, STATE:].reshape(blocks, BLOCK, STATE)
    scores = jnp.einsum('ktn,ksn->kts', c_narrow, b_narrow, preferred_element_type=jnp.float32)
    step_raw = jnp.dot(layer_in, weight_dt, preferred_element_type=jnp.float32) + bias_dt[None, :]
    values = ssm_in.astype(jnp.float32).reshape(length, HEADS, HEAD_DIM)
    primal, pull = jax.vjp(mixer, values, b_rows, c_rows, scores, step_raw, log_rate, skip_gain)
    cotangent = grad_out.astype(jnp.float32).reshape(length, HEADS, HEAD_DIM)
    grad_values, grad_b, grad_c, grad_scores, grad_step, grad_log_rate, grad_skip_gain = pull(cotangent)
    b_blocks = b_rows.reshape(blocks, BLOCK, STATE)
    c_blocks = c_rows.reshape(blocks, BLOCK, STATE)
    grad_b = grad_b + jnp.einsum('kts,ktn->ksn', grad_scores, c_blocks, precision=HIGHEST).reshape(length, STATE)
    grad_c = grad_c + jnp.einsum('kts,ksn->ktn', grad_scores, b_blocks, precision=HIGHEST).reshape(length, STATE)
    grad_bias_dt = lax.optimization_barrier(jnp.sum(grad_step, axis=0))
    grad_bc = jnp.concatenate([grad_b, grad_c], axis=1).astype(jnp.bfloat16)
    grad_dt = grad_step.astype(jnp.bfloat16)
    grad_layer_in = (jnp.dot(grad_bc, weight_bc.T, preferred_element_type=jnp.float32) + jnp.dot(grad_dt, weight_dt.T, preferred_element_type=jnp.float32)).astype(jnp.bfloat16)
    grad_weight_bc = jnp.dot(layer_in.T, grad_bc, preferred_element_type=jnp.float32)
    grad_weight_dt = jnp.dot(layer_in.T, grad_dt, preferred_element_type=jnp.float32)
    grad_ssm_in = grad_values.reshape(length, HEADS * HEAD_DIM).astype(jnp.bfloat16)
    return (grad_ssm_in, grad_layer_in, grad_weight_bc, grad_weight_dt, grad_bias_dt, grad_log_rate, grad_skip_gain)
```

```python
import functools
import jax
import jax.numpy as jnp
from jax import lax
from jax.experimental import pallas as pl
from jax.experimental.pallas import tpu as pltpu
from jax.sharding import PartitionSpec as P

F32 = jnp.float32
BF16 = jnp.bfloat16
TILE = 128
CHUNKS = 4
VMEM_LIMIT = 60 * 1024 * 1024
VMEM = pl.BlockSpec(memory_space=pltpu.VMEM)


def mm(left, right):
    return lax.dot_general(left, right, (((1,), (0,)), ((), ())), preferred_element_type=F32)


def mm_nt(left, right):
    return lax.dot_general(left, right, (((1,), (1,)), ((), ())), preferred_element_type=F32)


def mm_tn(left, right):
    return lax.dot_general(left, right, (((0,), (0,)), ((), ())), preferred_element_type=F32)


def three_way(x):
    high = x.astype(BF16)
    rest = x - high.astype(F32)
    middle = rest.astype(BF16)
    return high, middle, (rest - middle.astype(F32)).astype(BF16)


def one_hot(heads, width, columns, first=0):
    row = lax.broadcasted_iota(jnp.int32, (heads, columns), 0)
    col = lax.broadcasted_iota(jnp.int32, (heads, columns), 1) + first
    inside = (col >= row * width) & (col < (row + 1) * width)
    return jnp.where(inside, 1.0, 0.0).astype(BF16)


def spread_heads(x, hot):
    parts = three_way(x)
    return mm(parts[0], hot) + mm(parts[1], hot) + mm(parts[2], hot)


def head_sum(x, hot):
    high = x.astype(BF16)
    low = (x - high.astype(F32)).astype(BF16)
    return mm_nt(high, hot) + mm_nt(low, hot)


def exact_mm(mask, x):
    parts = three_way(x)
    return mm(mask, parts[0]) + mm(mask, parts[1]) + mm(mask, parts[2])


def triangle(size, compare):
    row = lax.broadcasted_iota(jnp.int32, (size, size), 0)
    col = lax.broadcasted_iota(jnp.int32, (size, size), 1)
    return jnp.where(compare(row, col), 1.0, 0.0).astype(BF16)


def before_kernel(
    layer_ref, values_ref, wbc_ref, wdt_ref, bias_ref, rate_ref, grad_ref,
    proj_ref, raw_ref, run_ref, run_rows_ref, states_ref, total_ref, scores_ref, skip_ref,
    u_ref, runx_ref,
):
    tokens = layer_ref.shape[0]
    heads = bias_ref.shape[1]
    width = values_ref.shape[1]
    head_size = width // heads
    state_dim = wbc_ref.shape[1] // 2
    layer = layer_ref[...]
    proj = mm(layer, wbc_ref[...]).astype(BF16)
    proj_ref[...] = proj
    b_rows = proj[:, :state_dim]
    c_rows = proj[:, state_dim:]
    scores_ref[...] = mm_nt(b_rows, c_rows)
    raw = mm(layer, wdt_ref[...]) + bias_ref[...]
    raw_ref[...] = raw
    step = jnp.maximum(raw, 0.0) + jnp.log1p(jnp.exp(-jnp.abs(raw)))
    decay = -jnp.exp(rate_ref[...]) * step
    run = exact_mm(triangle(tokens, lambda r, c: r >= c), decay)
    run_ref[...] = run
    run_rows = run.T
    for head in range(heads):
        run_rows_ref[head] = run_rows[head : head + 1]
    total = run[tokens - 1 :, :]
    total_ref[...] = jnp.zeros_like(total_ref)
    total_ref[:, :heads] = jnp.broadcast_to(total, (total_ref.shape[0], heads))
    hot = one_hot(heads, head_size, width)
    values = values_ref[...].astype(F32)
    grad = grad_ref[...].astype(F32)
    u_ref[...] = (spread_heads(step, hot) * values).astype(BF16)
    tail = spread_heads(jnp.exp(total - run) * step, hot)
    states_ref[0] = mm_tn(b_rows, (tail * values).astype(BF16))
    lead = spread_heads(jnp.exp(run), hot)
    states_ref[1] = mm_tn(c_rows, (lead * grad).astype(BF16))
    products = jnp.sum(values * grad, axis=0, keepdims=True)
    skip_ref[...] = head_sum(jnp.broadcast_to(products, (8, width)), hot)
    wide = one_hot(heads, TILE, heads * TILE)
    runx_ref[...] = spread_heads(run, wide)


def inner_pair(pair, values_ref, u_ref, grad_ref, scores_ref, runx_ref, run_rows_ref,
               gu_ref, rows_ref, gscores_ref, head_size):
    tokens = u_ref.shape[0]
    blocks = tokens // TILE
    per = TILE // head_size
    cols = pl.ds(pl.multiple_of(pair * TILE, TILE), TILE)
    lane = lax.broadcasted_iota(jnp.int32, (TILE, TILE), 1)
    causal = lax.broadcasted_iota(jnp.int32, (TILE, TILE), 0) <= lane
    grads = [grad_ref[t * TILE : (t + 1) * TILE, cols] for t in range(blocks)]
    gus = [jnp.zeros((TILE, TILE), F32) for _ in range(blocks)]
    for sub in range(per):
        head = pair * per + sub
        keep = (lane >= sub * head_size) & (lane < (sub + 1) * head_size)
        hcols = pl.ds(pl.multiple_of(head * TILE, TILE), TILE)
        rows = [jnp.zeros((1, TILE), F32) for _ in range(blocks)]
        for s in range(blocks):
            srange = slice(s * TILE, (s + 1) * TILE)
            run_col = runx_ref[srange, hcols]
            u_head = jnp.where(keep, u_ref[srange, cols], jnp.zeros((), BF16))
            gu = jnp.zeros((TILE, TILE), F32)
            for t in range(s, blocks):
                trange = slice(t * TILE, (t + 1) * TILE)
                gap = run_rows_ref[head, :, trange] - run_col
                if s == t:
                    gap = jnp.where(causal, gap, -jnp.inf)
                factor = jnp.exp(gap)
                mixing = (factor * scores_ref[srange, trange]).astype(BF16)
                weight = mm_nt(u_head, grads[t])
                gscores_ref[srange, trange] += factor * weight
                rows[t] += jnp.sum(mixing.astype(F32) * weight, axis=0, keepdims=True)
                gu += mm(mixing, grads[t])
            gus[s] = jnp.where(keep, gu, gus[s])
        for t in range(blocks):
            rows_ref[head, :, t * TILE : (t + 1) * TILE] = rows[t]
    for s in range(blocks):
        gu_ref[s * TILE : (s + 1) * TILE, cols] = gus[s]


def inner_kernel(head_size, u_ref, grad_ref, scores_ref, runx_ref, run_rows_ref,
                 gu_ref, rows_ref, gscores_ref):
    gscores_ref[...] = jnp.zeros_like(gscores_ref)

    def body(pair, _):
        inner_pair(pair, None, u_ref, grad_ref, scores_ref, runx_ref, run_rows_ref,
                   gu_ref, rows_ref, gscores_ref, head_size)
        return 0

    lax.fori_loop(0, u_ref.shape[1] // TILE, body, 0)


def scan_plan(devices, rows):
    levels = devices.bit_length() - 1
    sizes, halved = [rows], []
    for level in range(levels - 1):
        cut = sizes[-1] >= 16
        halved.append(cut)
        sizes.append(sizes[-1] // 2 if cut else sizes[-1])
    return levels, sizes, halved


def scan_kernel(devices, heads, states_ref, total_ref, out_ref, *refs):
    rows, width = states_ref.shape[1], states_ref.shape[2]
    head_size = width // heads
    levels, sizes, halved = scan_plan(devices, rows)
    top = levels - 1
    refs = list(refs)
    aggs = [states_ref] + [refs.pop(0) for _ in range(top)]
    gets = [refs.pop(0) for _ in range(top)]
    outs = [out_ref] + [refs.pop(0) for _ in range(top)]
    sends = [refs.pop(0) if halved[k] else None for k in range(top)]
    downs = [refs.pop(0) if halved[k] else None for k in range(top)]
    top_get, tots, tot_gets, decays, up_sems, down_sems, tot_sems = refs
    me = lax.axis_index("seq")
    bits = [lax.rem(me // (1 << k), 2) for k in range(levels)]
    partners = [me + (1 - 2 * bits[k]) * (1 << k) for k in range(levels)]
    barrier = pltpu.get_barrier_semaphore()
    for k in range(levels):
        pl.semaphore_signal(
            barrier, inc=1, device_id={"seq": partners[k]}, device_id_type=pl.DeviceIdType.MESH
        )
    pl.semaphore_wait(barrier, levels)
    span = width // CHUNKS

    def copy(source, target, send, receive, k):
        return pltpu.make_async_remote_copy(
            src_ref=source, dst_ref=target, send_sem=send, recv_sem=receive,
            device_id={"seq": partners[k]}, device_id_type=pl.DeviceIdType.MESH,
        )

    def half_at(k, which):
        size = sizes[k + 1]
        return pl.ds(pl.multiple_of(which * size, 8), size)

    def up_copy(k, c):
        cols = slice(c * span, (c + 1) * span)
        if k == top:
            source, target = aggs[k].at[bits[k], :, cols], top_get.at[:, cols]
        elif halved[k]:
            source, target = aggs[k].at[:, half_at(k, 1 - bits[k]), cols], gets[k].at[:, :, cols]
        else:
            source, target = aggs[k].at[:, :, cols], gets[k].at[:, :, cols]
        return copy(source, target, up_sems.at[0, k, c], up_sems.at[1, k, c], k)

    def down_copy(k, c):
        cols = slice(c * span, (c + 1) * span)
        return copy(sends[k].at[:, :, cols], downs[k].at[:, :, cols],
                    down_sems.at[0, k, c], down_sems.at[1, k, c], k)

    def tot_copy(k):
        return copy(tots.at[k], tot_gets.at[k], tot_sems.at[0, k], tot_sems.at[1, k], k)

    def tot_done(k):
        tot_copy(k).wait_recv()
        mine, other = tots[k], tot_gets[k]
        tots[k + 1] = mine + other
        left = jnp.where(bits[k] == 0, mine, other)
        right = jnp.where(bits[k] == 0, other, mine)
        hot = one_hot(TILE, head_size, width)
        decays[k, 0] = jnp.exp(spread_heads(left, hot))
        decays[k, 1] = jnp.exp(spread_heads(right, hot))

    def own(k, cols, part):
        if halved[k]:
            return aggs[k][part, half_at(k, bits[k]), cols]
        return aggs[k][part, :, cols]

    def finish_up(k, c):
        cols = slice(c * span, (c + 1) * span)
        up_copy(k, c).wait_recv()
        if c == 0:
            tot_done(k)
            if k + 1 < top:
                tot_copy(k + 1).start()
        first = bits[k] == 0
        s_mine, g_mine = own(k, cols, 0), own(k, cols, 1)
        s_got, g_got = gets[k][0, :, cols], gets[k][1, :, cols]
        s_left, s_right = jnp.where(first, s_mine, s_got), jnp.where(first, s_got, s_mine)
        g_left, g_right = jnp.where(first, g_mine, g_got), jnp.where(first, g_got, g_mine)
        aggs[k + 1][0, :, cols] = decays[k, 1, 0:1, cols] * s_left + s_right
        aggs[k + 1][1, :, cols] = g_left + decays[k, 0, 0:1, cols] * g_right
        up_copy(k + 1, c).start()

    def finish_top(c):
        cols = slice(c * span, (c + 1) * span)
        up_copy(top, c).wait_recv()
        got = top_get[:, cols]
        zero = jnp.zeros_like(got)
        outs[top][0, :, cols] = jnp.where(bits[top] == 1, got, zero)
        outs[top][1, :, cols] = jnp.where(bits[top] == 1, zero, got)
        if top > 0:
            step_down(top - 1, c)

    def step_down(k, c):
        cols = slice(c * span, (c + 1) * span)
        first = bits[k] == 0
        inc, outg = outs[k + 1][0, :, cols], outs[k + 1][1, :, cols]
        s_left = jnp.where(first, own(k, cols, 0), gets[k][0, :, cols])
        g_right = jnp.where(first, gets[k][1, :, cols], own(k, cols, 1))
        right_in = decays[k, 0, 0:1, cols] * inc + s_left
        left_out = decays[k, 1, 0:1, cols] * outg + g_right
        if halved[k]:
            sends[k][0, :, cols] = jnp.where(first, right_in, inc)
            sends[k][1, :, cols] = jnp.where(first, outg, left_out)
            down_copy(k, c).start()
            mine = half_at(k, bits[k])
        else:
            mine = slice(None)
        outs[k][0, mine, cols] = jnp.where(first, inc, right_in)
        outs[k][1, mine, cols] = jnp.where(first, left_out, outg)

    def finish_down(k, c):
        cols = slice(c * span, (c + 1) * span)
        if halved[k]:
            down_copy(k, c).wait_recv()
            outs[k][:, half_at(k, 1 - bits[k]), cols] = downs[k][:, :, cols]
        if k > 0:
            step_down(k - 1, c)

    tots[0] = total_ref[...]
    if top > 0:
        tot_copy(0).start()
    for c in range(CHUNKS):
        up_copy(0, c).start()
    stages = [functools.partial(finish_up, k) for k in range(top)]
    stages.append(finish_top)
    stages += [functools.partial(finish_down, k) for k in reversed(range(top))]
    for tick in range(len(stages) + CHUNKS - 1):
        for c in range(CHUNKS):
            if 0 <= tick - c < len(stages):
                stages[tick - c](c)
    for k in range(top):
        tot_copy(k).wait_send()
    for c in range(CHUNKS):
        for k in range(levels):
            up_copy(k, c).wait_send()
        for k in range(top):
            if halved[k]:
                down_copy(k, c).wait_send()


def scan_states(devices, heads, states, total):
    rows, width = states.shape[1], states.shape[2]
    levels, sizes, halved = scan_plan(devices, rows)
    top = levels - 1
    scratch = [pltpu.VMEM((2, sizes[k + 1], width), F32) for k in range(top)]
    scratch += [pltpu.VMEM((2, sizes[k + 1], width), F32) for k in range(top)]
    scratch += [pltpu.VMEM((2, sizes[k + 1], width), F32) for k in range(top)]
    for _ in range(2):
        scratch += [pltpu.VMEM((2, sizes[k + 1], width), F32) for k in range(top) if halved[k]]
    scratch += [
        pltpu.VMEM((sizes[top], width), F32),
        pltpu.VMEM((levels + 1, 8, TILE), F32),
        pltpu.VMEM((levels, 8, TILE), F32),
        pltpu.VMEM((levels, 2, 8, width), F32),
        pltpu.SemaphoreType.DMA((2, levels, CHUNKS)),
        pltpu.SemaphoreType.DMA((2, levels, CHUNKS)),
        pltpu.SemaphoreType.DMA((2, levels)),
    ]
    return pl.pallas_call(
        functools.partial(scan_kernel, devices, heads),
        out_shape=jax.ShapeDtypeStruct(states.shape, F32),
        in_specs=[VMEM, VMEM],
        out_specs=VMEM,
        scratch_shapes=scratch,
        compiler_params=pltpu.CompilerParams(
            collective_id=0, has_side_effects=True, vmem_limit_bytes=VMEM_LIMIT
        ),
        name="scan_states",
    )(states, total)


def after_kernel(
    values_ref, grad_ref, proj_ref, raw_ref, run_ref, u_ref, rate_ref, skip_ref,
    gu_ref, rows_ref, gscores_ref, ends_ref, wbc_ref, wdt_ref,
    gvalues_ref, glayer_ref, gproj_ref, small_ref,
):
    tokens, heads = raw_ref.shape
    width = values_ref.shape[1]
    head_size = width // heads
    state_dim = proj_ref.shape[1] // 2
    hot = one_hot(heads, head_size, width)
    raw, run = raw_ref[...], run_ref[...]
    rate = jnp.exp(rate_ref[...])
    step = jnp.maximum(raw, 0.0) + jnp.log1p(jnp.exp(-jnp.abs(raw)))
    total = run[tokens - 1 :, :]
    b_rows = proj_ref[:, :state_dim]
    c_rows = proj_ref[:, state_dim:]
    incoming, outgoing = ends_ref[0], ends_ref[1]
    inc_b, out_b = incoming.astype(BF16), outgoing.astype(BF16)
    values = values_ref[...].astype(F32)
    grad = grad_ref[...].astype(F32)
    step_wide = spread_heads(step, hot)
    lead_grad = spread_heads(jnp.exp(run), hot) * grad
    lead_b = lead_grad.astype(BF16)
    reads = head_sum(lead_grad * mm(c_rows, inc_b), hot)
    gscores = gscores_ref[...].astype(BF16)
    grad_c = mm_nt(lead_b, inc_b) + mm_tn(gscores, b_rows)
    tail_wide = spread_heads(jnp.exp(total - run), hot)
    back = tail_wide * mm(b_rows, out_b)
    grad_b = mm_nt((tail_wide * step_wide * values).astype(BF16), out_b) + mm(gscores, c_rows)
    gu = gu_ref[...]
    inner_cols = head_sum(u_ref[...].astype(F32) * gu, hot)
    back_sum = head_sum(values * back, hot)
    gu = gu + back
    gvalues_ref[...] = (step_wide * gu + spread_heads(skip_ref[...], hot) * grad).astype(BF16)
    grad_step = head_sum(values * gu, hot)
    cross = jnp.sum(incoming * outgoing, axis=0, keepdims=True)
    cross = head_sum(jnp.broadcast_to(cross, (8, width)), hot)[0:1]
    upper = triangle(tokens, lambda r, c: r <= c)
    lower = triangle(tokens, lambda r, c: r > c)
    inner = rows_ref[:, 0, :].T + reads - inner_cols
    grad_decay = exact_mm(upper, inner) + exact_mm(lower, step * back_sum) + jnp.exp(total) * cross
    sigmoid = 1.0 / (1.0 + jnp.exp(-raw))
    grad_raw = (grad_step - rate * grad_decay) * sigmoid
    gproj_ref[:, :state_dim] = grad_b.astype(BF16)
    gproj_ref[:, state_dim : 2 * state_dim] = grad_c.astype(BF16)
    gproj_ref[:, 2 * state_dim :] = grad_raw.astype(BF16)
    small_ref[...] = jnp.zeros_like(small_ref)
    small_ref[0:1] = jnp.sum(grad_raw, axis=0, keepdims=True)
    small_ref[1:2] = -rate * jnp.sum(grad_decay * step, axis=0, keepdims=True)
    glayer_ref[...] = (
        mm_nt(gproj_ref[:, : 2 * state_dim], wbc_ref[...])
        + mm_nt(grad_raw.astype(BF16), wdt_ref[...])
    ).astype(BF16)


def call(kernel, shapes, name, *operands):
    return pl.pallas_call(
        kernel,
        out_shape=[jax.ShapeDtypeStruct(shape, dtype) for shape, dtype in shapes],
        in_specs=[VMEM] * len(operands),
        out_specs=[VMEM] * len(shapes),
        compiler_params=pltpu.CompilerParams(vmem_limit_bytes=VMEM_LIMIT),
        name=name,
    )(*operands)


def local(layer_in, ssm_in, weight_bc, weight_dt, bias_dt, log_rate, skip_gain, grad_out):
    tokens, depth = layer_in.shape
    heads = log_rate.shape[0]
    width = ssm_in.shape[1]
    state_dim = weight_bc.shape[1] // 2
    head_size = width // heads
    devices = lax.axis_size("seq")
    bias, rate, gain = bias_dt[None, :], log_rate[None, :], skip_gain[None, :]
    proj, raw, run, run_rows, states, total, scores, skip_sum, u, runx = call(
        before_kernel,
        [
            ((tokens, 2 * state_dim), BF16),
            ((tokens, heads), F32),
            ((tokens, heads), F32),
            ((heads, 1, tokens), F32),
            ((2, state_dim, width), F32),
            ((8, TILE), F32),
            ((tokens, tokens), F32),
            ((8, heads), F32),
            ((tokens, width), BF16),
            ((tokens, heads * TILE), F32),
        ],
        "before",
        layer_in, ssm_in, weight_bc, weight_dt, bias, rate, grad_out,
    )
    ends = scan_states(devices, heads, states, total)
    gu, rows, gscores = call(
        functools.partial(inner_kernel, head_size),
        [((tokens, width), F32), ((heads, 1, tokens), F32), ((tokens, tokens), F32)],
        "inner",
        u, grad_out, scores, runx, run_rows,
    )
    grad_ssm_in, grad_layer_in, grad_proj, small = call(
        after_kernel,
        [
            ((tokens, width), BF16),
            ((tokens, depth), BF16),
            ((tokens, 2 * state_dim + heads), BF16),
            ((8, heads), F32),
        ],
        "after",
        ssm_in, grad_out, proj, raw, run, u, rate, gain, gu, rows, gscores, ends,
        weight_bc, weight_dt,
    )
    grad_rows = lax.dot_general(
        layer_in, grad_proj, (((0,), (0,)), ((), ())), preferred_element_type=F32
    )
    share = depth // devices
    columns = grad_rows.shape[1]
    small = jnp.concatenate([small[0:2], skip_sum[0:1]], axis=0)
    small = jnp.pad(small, ((0, 5), (0, columns - heads)))
    packed = jnp.concatenate(
        [
            grad_rows.reshape(devices, share, columns),
            jnp.broadcast_to(small[None], (devices, 8, columns)),
        ],
        axis=1,
    ).reshape(devices * (share + 8), columns)
    summed = lax.psum_scatter(packed, "seq", scatter_dimension=0, tiled=True)
    return (
        grad_ssm_in,
        grad_layer_in,
        summed[:share, : 2 * state_dim],
        summed[:share, 2 * state_dim :],
        summed[share, :heads],
        summed[share + 1, :heads],
        summed[share + 2, :heads],
    )


def solution(mesh):
    rows = P(("groups", "seq"), None)
    in_specs = (rows, rows, P(), P(), P(), P(), P(), rows)
    out_specs = (rows, rows, rows, rows, P("groups"), P("groups"), P("groups"))
    return jax.shard_map(local, mesh=mesh, in_specs=in_specs, out_specs=out_specs, check_vma=False)
```

```python
import functools
import jax
import jax.numpy as jnp
from jax import lax
from jax.experimental import pallas as pl
from jax.experimental.pallas import tpu as pltpu
from jax.sharding import PartitionSpec as P

F32 = jnp.float32
BF16 = jnp.bfloat16
TILE = 128
CHUNKS = 4
VMEM_LIMIT = 60 * 1024 * 1024
VMEM = pl.BlockSpec(memory_space=pltpu.VMEM)


def mm(left, right):
    return lax.dot_general(left, right, (((1,), (0,)), ((), ())), preferred_element_type=F32)


def mm_nt(left, right):
    return lax.dot_general(left, right, (((1,), (1,)), ((), ())), preferred_element_type=F32)


def mm_tn(left, right):
    return lax.dot_general(left, right, (((0,), (0,)), ((), ())), preferred_element_type=F32)


def three_way(x):
    high = x.astype(BF16)
    rest = x - high.astype(F32)
    middle = rest.astype(BF16)
    return high, middle, (rest - middle.astype(F32)).astype(BF16)


def one_hot(heads, width, columns, first=0):
    row = lax.broadcasted_iota(jnp.int32, (heads, columns), 0)
    col = lax.broadcasted_iota(jnp.int32, (heads, columns), 1) + first
    inside = (col >= row * width) & (col < (row + 1) * width)
    return jnp.where(inside, 1.0, 0.0).astype(BF16)


def spread_heads(x, hot):
    parts = three_way(x)
    return mm(parts[0], hot) + mm(parts[1], hot) + mm(parts[2], hot)


def head_sum(x, hot):
    high = x.astype(BF16)
    low = (x - high.astype(F32)).astype(BF16)
    return mm_nt(high, hot) + mm_nt(low, hot)


def exact_mm(mask, x):
    parts = three_way(x)
    return mm(mask, parts[0]) + mm(mask, parts[1]) + mm(mask, parts[2])


def triangle(size, compare):
    row = lax.broadcasted_iota(jnp.int32, (size, size), 0)
    col = lax.broadcasted_iota(jnp.int32, (size, size), 1)
    return jnp.where(compare(row, col), 1.0, 0.0).astype(BF16)


def before_kernel(
    layer_ref, values_ref, wbc_ref, wdt_ref, bias_ref, rate_ref, grad_ref,
    proj_ref, raw_ref, run_ref, run_rows_ref, states_ref, total_ref, scores_ref, skip_ref,
    u_ref, runx_ref,
):
    tokens = layer_ref.shape[0]
    heads = bias_ref.shape[1]
    width = values_ref.shape[1]
    head_size = width // heads
    state_dim = wbc_ref.shape[1] // 2
    layer = layer_ref[...]
    proj = mm(layer, wbc_ref[...]).astype(BF16)
    proj_ref[...] = proj
    b_rows = proj[:, :state_dim]
    c_rows = proj[:, state_dim:]
    scores_ref[...] = mm_nt(b_rows, c_rows)
    raw = mm(layer, wdt_ref[...]) + bias_ref[...]
    raw_ref[...] = raw
    step = jnp.maximum(raw, 0.0) + jnp.log1p(jnp.exp(-jnp.abs(raw)))
    decay = -jnp.exp(rate_ref[...]) * step
    run = exact_mm(triangle(tokens, lambda r, c: r >= c), decay)
    run_ref[...] = run
    run_rows = run.T
    for head in range(heads):
        run_rows_ref[head] = run_rows[head : head + 1]
    total = run[tokens - 1 :, :]
    total_ref[...] = jnp.zeros_like(total_ref)
    total_ref[:, :heads] = jnp.broadcast_to(total, (total_ref.shape[0], heads))
    hot = one_hot(heads, head_size, width)
    values = values_ref[...].astype(F32)
    grad = grad_ref[...].astype(F32)
    u_ref[...] = (spread_heads(step, hot) * values).astype(BF16)
    tail = spread_heads(jnp.exp(total - run) * step, hot)
    states_ref[0] = mm_tn(b_rows, (tail * values).astype(BF16))
    lead = spread_heads(jnp.exp(run), hot)
    states_ref[1] = mm_tn(c_rows, (lead * grad).astype(BF16))
    products = jnp.sum(values * grad, axis=0, keepdims=True)
    skip_ref[...] = head_sum(jnp.broadcast_to(products, (8, width)), hot)
    wide = one_hot(heads, TILE, heads * TILE)
    runx_ref[...] = spread_heads(run, wide)


def inner_pair(pair, values_ref, u_ref, grad_ref, scores_ref, runx_ref, run_rows_ref,
               gu_ref, rows_ref, gscores_ref, head_size):
    tokens = u_ref.shape[0]
    blocks = tokens // TILE
    per = TILE // head_size
    cols = pl.ds(pl.multiple_of(pair * TILE, TILE), TILE)
    lane = lax.broadcasted_iota(jnp.int32, (TILE, TILE), 1)
    causal = lax.broadcasted_iota(jnp.int32, (TILE, TILE), 0) <= lane
    grads = [grad_ref[t * TILE : (t + 1) * TILE, cols] for t in range(blocks)]
    gus = [jnp.zeros((TILE, TILE), F32) for _ in range(blocks)]
    for sub in range(per):
        head = pair * per + sub
        keep = (lane >= sub * head_size) & (lane < (sub + 1) * head_size)
        hcols = pl.ds(pl.multiple_of(head * TILE, TILE), TILE)
        rows = [jnp.zeros((1, TILE), F32) for _ in range(blocks)]
        for s in range(blocks):
            srange = slice(s * TILE, (s + 1) * TILE)
            run_col = runx_ref[srange, hcols]
            u_head = jnp.where(keep, u_ref[srange, cols], jnp.zeros((), BF16))
            gu = jnp.zeros((TILE, TILE), F32)
            for t in range(s, blocks):
                trange = slice(t * TILE, (t + 1) * TILE)
                gap = run_rows_ref[head, :, trange] - run_col
                if s == t:
                    gap = jnp.where(causal, gap, -jnp.inf)
                factor = jnp.exp(gap)
                mixing = (factor * scores_ref[srange, trange]).astype(BF16)
                weight = mm_nt(u_head, grads[t])
                gscores_ref[srange, trange] += factor * weight
                rows[t] += jnp.sum(mixing.astype(F32) * weight, axis=0, keepdims=True)
                gu += mm(mixing, grads[t])
            gus[s] = jnp.where(keep, gu, gus[s])
        for t in range(blocks):
            rows_ref[head, :, t * TILE : (t + 1) * TILE] = rows[t]
    for s in range(blocks):
        gu_ref[s * TILE : (s + 1) * TILE, cols] = gus[s]


def inner_kernel(head_size, u_ref, grad_ref, scores_ref, runx_ref, run_rows_ref,
                 gu_ref, rows_ref, gscores_ref):
    gscores_ref[...] = jnp.zeros_like(gscores_ref)

    def body(pair, _):
        inner_pair(pair, None, u_ref, grad_ref, scores_ref, runx_ref, run_rows_ref,
                   gu_ref, rows_ref, gscores_ref, head_size)
        return 0

    lax.fori_loop(0, u_ref.shape[1] // TILE, body, 0)


def scan_plan(devices, rows):
    levels = devices.bit_length() - 1
    sizes, halved = [rows], []
    for level in range(levels - 1):
        cut = sizes[-1] >= 16
        halved.append(cut)
        sizes.append(sizes[-1] // 2 if cut else sizes[-1])
    return levels, sizes, halved


def scan_kernel(devices, heads, states_ref, total_ref, out_ref, *refs):
    rows, width = states_ref.shape[1], states_ref.shape[2]
    head_size = width // heads
    levels, sizes, halved = scan_plan(devices, rows)
    top = levels - 1
    refs = list(refs)
    aggs = [states_ref] + [refs.pop(0) for _ in range(top)]
    gets = [refs.pop(0) for _ in range(top)]
    outs = [out_ref] + [refs.pop(0) for _ in range(top)]
    sends = [refs.pop(0) if halved[k] else None for k in range(top)]
    downs = [refs.pop(0) if halved[k] else None for k in range(top)]
    top_get, tots, tot_gets, decays, up_sems, down_sems, tot_sems = refs
    me = lax.axis_index("seq")
    bits = [lax.rem(me // (1 << k), 2) for k in range(levels)]
    partners = [me + (1 - 2 * bits[k]) * (1 << k) for k in range(levels)]
    barrier = pltpu.get_barrier_semaphore()
    for k in range(levels):
        pl.semaphore_signal(
            barrier, inc=1, device_id={"seq": partners[k]}, device_id_type=pl.DeviceIdType.MESH
        )
    pl.semaphore_wait(barrier, levels)
    span = width // CHUNKS

    def copy(source, target, send, receive, k):
        return pltpu.make_async_remote_copy(
            src_ref=source, dst_ref=target, send_sem=send, recv_sem=receive,
            device_id={"seq": partners[k]}, device_id_type=pl.DeviceIdType.MESH,
        )

    def half_at(k, which):
        size = sizes[k + 1]
        return pl.ds(pl.multiple_of(which * size, 8), size)

    def up_copy(k, c):
        cols = slice(c * span, (c + 1) * span)
        if k == top:
            source, target = aggs[k].at[bits[k], :, cols], top_get.at[:, cols]
        elif halved[k]:
            source, target = aggs[k].at[:, half_at(k, 1 - bits[k]), cols], gets[k].at[:, :, cols]
        else:
            source, target = aggs[k].at[:, :, cols], gets[k].at[:, :, cols]
        return copy(source, target, up_sems.at[0, k, c], up_sems.at[1, k, c], k)

    def down_copy(k, c):
        cols = slice(c * span, (c + 1) * span)
        return copy(sends[k].at[:, :, cols], downs[k].at[:, :, cols],
                    down_sems.at[0, k, c], down_sems.at[1, k, c], k)

    def tot_copy(k):
        return copy(tots.at[k], tot_gets.at[k], tot_sems.at[0, k], tot_sems.at[1, k], k)

    def tot_done(k):
        tot_copy(k).wait_recv()
        mine, other = tots[k], tot_gets[k]
        tots[k + 1] = mine + other
        left = jnp.where(bits[k] == 0, mine, other)
        right = jnp.where(bits[k] == 0, other, mine)
        hot = one_hot(TILE, head_size, width)
        decays[k, 0] = jnp.exp(spread_heads(left, hot))
        decays[k, 1] = jnp.exp(spread_heads(right, hot))

    def own(k, cols, part):
        if halved[k]:
            return aggs[k][part, half_at(k, bits[k]), cols]
        return aggs[k][part, :, cols]

    def finish_up(k, c):
        cols = slice(c * span, (c + 1) * span)
        up_copy(k, c).wait_recv()
        if c == 0:
            tot_done(k)
            if k + 1 < top:
                tot_copy(k + 1).start()
        first = bits[k] == 0
        s_mine, g_mine = own(k, cols, 0), own(k, cols, 1)
        s_got, g_got = gets[k][0, :, cols], gets[k][1, :, cols]
        s_left, s_right = jnp.where(first, s_mine, s_got), jnp.where(first, s_got, s_mine)
        g_left, g_right = jnp.where(first, g_mine, g_got), jnp.where(first, g_got, g_mine)
        aggs[k + 1][0, :, cols] = decays[k, 1, 0:1, cols] * s_left + s_right
        aggs[k + 1][1, :, cols] = g_left + decays[k, 0, 0:1, cols] * g_right
        up_copy(k + 1, c).start()

    def finish_top(c):
        cols = slice(c * span, (c + 1) * span)
        up_copy(top, c).wait_recv()
        got = top_get[:, cols]
        zero = jnp.zeros_like(got)
        outs[top][0, :, cols] = jnp.where(bits[top] == 1, got, zero)
        outs[top][1, :, cols] = jnp.where(bits[top] == 1, zero, got)
        if top > 0:
            step_down(top - 1, c)

    def step_down(k, c):
        cols = slice(c * span, (c + 1) * span)
        first = bits[k] == 0
        inc, outg = outs[k + 1][0, :, cols], outs[k + 1][1, :, cols]
        s_left = jnp.where(first, own(k, cols, 0), gets[k][0, :, cols])
        g_right = jnp.where(first, gets[k][1, :, cols], own(k, cols, 1))
        right_in = decays[k, 0, 0:1, cols] * inc + s_left
        left_out = decays[k, 1, 0:1, cols] * outg + g_right
        if halved[k]:
            sends[k][0, :, cols] = jnp.where(first, right_in, inc)
            sends[k][1, :, cols] = jnp.where(first, outg, left_out)
            down_copy(k, c).start()
            mine = half_at(k, bits[k])
        else:
            mine = slice(None)
        outs[k][0, mine, cols] = jnp.where(first, inc, right_in)
        outs[k][1, mine, cols] = jnp.where(first, left_out, outg)

    def finish_down(k, c):
        cols = slice(c * span, (c + 1) * span)
        if halved[k]:
            down_copy(k, c).wait_recv()
            outs[k][:, half_at(k, 1 - bits[k]), cols] = downs[k][:, :, cols]
        if k > 0:
            step_down(k - 1, c)

    tots[0] = total_ref[...]
    if top > 0:
        tot_copy(0).start()
    for c in range(CHUNKS):
        up_copy(0, c).start()
    stages = [functools.partial(finish_up, k) for k in range(top)]
    stages.append(finish_top)
    stages += [functools.partial(finish_down, k) for k in reversed(range(top))]
    for tick in range(len(stages) + CHUNKS - 1):
        for c in range(CHUNKS):
            if 0 <= tick - c < len(stages):
                stages[tick - c](c)
    for k in range(top):
        tot_copy(k).wait_send()
    for c in range(CHUNKS):
        for k in range(levels):
            up_copy(k, c).wait_send()
        for k in range(top):
            if halved[k]:
                down_copy(k, c).wait_send()


def scan_states(devices, heads, states, total):
    rows, width = states.shape[1], states.shape[2]
    levels, sizes, halved = scan_plan(devices, rows)
    top = levels - 1
    scratch = [pltpu.VMEM((2, sizes[k + 1], width), F32) for k in range(top)]
    scratch += [pltpu.VMEM((2, sizes[k + 1], width), F32) for k in range(top)]
    scratch += [pltpu.VMEM((2, sizes[k + 1], width), F32) for k in range(top)]
    for _ in range(2):
        scratch += [pltpu.VMEM((2, sizes[k + 1], width), F32) for k in range(top) if halved[k]]
    scratch += [
        pltpu.VMEM((sizes[top], width), F32),
        pltpu.VMEM((levels + 1, 8, TILE), F32),
        pltpu.VMEM((levels, 8, TILE), F32),
        pltpu.VMEM((levels, 2, 8, width), F32),
        pltpu.SemaphoreType.DMA((2, levels, CHUNKS)),
        pltpu.SemaphoreType.DMA((2, levels, CHUNKS)),
        pltpu.SemaphoreType.DMA((2, levels)),
    ]
    return pl.pallas_call(
        functools.partial(scan_kernel, devices, heads),
        out_shape=jax.ShapeDtypeStruct(states.shape, F32),
        in_specs=[VMEM, VMEM],
        out_specs=VMEM,
        scratch_shapes=scratch,
        compiler_params=pltpu.CompilerParams(
            collective_id=0, has_side_effects=True, vmem_limit_bytes=VMEM_LIMIT
        ),
        name="scan_states",
    )(states, total)


def after_kernel(
    values_ref, grad_ref, proj_ref, raw_ref, run_ref, u_ref, rate_ref, skip_ref,
    gu_ref, rows_ref, gscores_ref, ends_ref, wbc_ref, wdt_ref, skip_sum_ref,
    gvalues_ref, glayer_ref, gproj_ref, small_ref,
):
    tokens, heads = raw_ref.shape
    width = values_ref.shape[1]
    head_size = width // heads
    state_dim = proj_ref.shape[1] // 2
    hot = one_hot(heads, head_size, width)
    raw, run = raw_ref[...], run_ref[...]
    rate = jnp.exp(rate_ref[...])
    step = jnp.maximum(raw, 0.0) + jnp.log1p(jnp.exp(-jnp.abs(raw)))
    total = run[tokens - 1 :, :]
    b_rows = proj_ref[:, :state_dim]
    c_rows = proj_ref[:, state_dim:]
    incoming, outgoing = ends_ref[0], ends_ref[1]
    inc_b, out_b = incoming.astype(BF16), outgoing.astype(BF16)
    values = values_ref[...].astype(F32)
    grad = grad_ref[...].astype(F32)
    step_wide = spread_heads(step, hot)
    lead_grad = spread_heads(jnp.exp(run), hot) * grad
    lead_b = lead_grad.astype(BF16)
    reads = head_sum(lead_grad * mm(c_rows, inc_b), hot)
    gscores = gscores_ref[...].astype(BF16)
    grad_c = mm_nt(lead_b, inc_b) + mm_tn(gscores, b_rows)
    tail_wide = spread_heads(jnp.exp(total - run), hot)
    back = tail_wide * mm(b_rows, out_b)
    grad_b = mm_nt((tail_wide * step_wide * values).astype(BF16), out_b) + mm(gscores, c_rows)
    gu = gu_ref[...]
    inner_cols = head_sum(u_ref[...].astype(F32) * gu, hot)
    back_sum = head_sum(values * back, hot)
    gu = gu + back
    gvalues_ref[...] = (step_wide * gu + spread_heads(skip_ref[...], hot) * grad).astype(BF16)
    grad_step = head_sum(values * gu, hot)
    cross = jnp.sum(incoming * outgoing, axis=0, keepdims=True)
    cross = head_sum(jnp.broadcast_to(cross, (8, width)), hot)[0:1]
    upper = triangle(tokens, lambda r, c: r <= c)
    lower = triangle(tokens, lambda r, c: r > c)
    inner = rows_ref[:, 0, :].T + reads - inner_cols
    grad_decay = exact_mm(upper, inner) + exact_mm(lower, step * back_sum) + jnp.exp(total) * cross
    sigmoid = 1.0 / (1.0 + jnp.exp(-raw))
    grad_raw = (grad_step - rate * grad_decay) * sigmoid
    gproj_ref[:, :state_dim] = grad_b.astype(BF16)
    gproj_ref[:, state_dim : 2 * state_dim] = grad_c.astype(BF16)
    gproj_ref[:, 2 * state_dim :] = grad_raw.astype(BF16)
    small_ref[...] = jnp.zeros_like(small_ref)
    small_ref[0:1, :heads] = jnp.sum(grad_raw, axis=0, keepdims=True)
    small_ref[1:2, :heads] = -rate * jnp.sum(grad_decay * step, axis=0, keepdims=True)
    small_ref[2:3, :heads] = skip_sum_ref[0:1]
    glayer_ref[...] = (
        mm_nt(gproj_ref[:, : 2 * state_dim], wbc_ref[...])
        + mm_nt(grad_raw.astype(BF16), wdt_ref[...])
    ).astype(BF16)


def packing(depth, devices, heads):
    share = depth // devices
    lanes = TILE // heads
    group = -(-share // (8 * lanes)) * 8
    return share, lanes, group


def reduce_kernel(devices, heads, layer_ref, gproj_ref, small_ref,
                  gbc_ref, gdt_ref, gbias_ref, grate_ref, gskip_ref, *refs):
    depth = layer_ref.shape[1]
    share, lanes, group = packing(depth, devices, heads)
    levels = devices.bit_length() - 1
    wide = gbc_ref.shape[1]
    planes = wide // TILE + 1
    refs = list(refs)
    sems = refs.pop()
    sums = [refs.pop(0) for _ in range(planes)]
    gets = [[refs.pop(0) for _ in range(levels)] for _ in range(planes)]
    units = [share] * (planes - 1) + [group + 8]
    me = lax.axis_index("seq")
    bits = [lax.rem(me // (1 << k), 2) for k in range(levels)]
    partners = [me + (1 - 2 * bits[k]) * (1 << k) for k in range(levels)]
    offsets = [0]
    for k in range(levels):
        offsets.append(offsets[k] + bits[k] * (devices >> (k + 1)))
    barrier = pltpu.get_barrier_semaphore()
    for k in range(levels):
        pl.semaphore_signal(
            barrier, inc=1, device_id={"seq": partners[k]}, device_id_type=pl.DeviceIdType.MESH
        )
    pl.semaphore_wait(barrier, levels)
    places = [
        sum(((shard >> k) & 1) * (devices >> (k + 1)) for k in range(levels))
        for shard in range(devices)
    ]

    def half(k, plane, which):
        size = (devices >> (k + 1)) * units[plane]
        start = (offsets[k] + which * (devices >> (k + 1))) * units[plane]
        return pl.ds(pl.multiple_of(start, 8), size)

    def copy(k, plane):
        return pltpu.make_async_remote_copy(
            src_ref=sums[plane].at[half(k, plane, 1 - bits[k])],
            dst_ref=gets[plane][k],
            send_sem=sems.at[0, k, plane],
            recv_sem=sems.at[1, k, plane],
            device_id={"seq": partners[k]},
            device_id_type=pl.DeviceIdType.MESH,
        )

    layer = layer_ref[...]
    rows_bc = mm_tn(layer, gproj_ref[:, :wide])
    for plane in range(planes - 1):
        for shard in range(devices):
            sums[plane][places[shard] * share : (places[shard] + 1) * share] = rows_bc[
                shard * share : (shard + 1) * share, plane * TILE : (plane + 1) * TILE
            ]
        copy(0, plane).start()
    row = lax.broadcasted_iota(jnp.int32, (heads, lanes * TILE), 0)
    col = lax.broadcasted_iota(jnp.int32, (heads, lanes * TILE), 1)
    shift = jnp.zeros(row.shape, F32)
    for j in range(lanes):
        shift = jnp.where(col == row + j * (TILE + heads), 1.0, shift)
    moved = mm(gproj_ref[:, wide:], shift.astype(BF16)).astype(BF16)
    rows_dt = mm_tn(layer, moved)
    unit = group + 8
    for shard in range(devices):
        start = places[shard] * unit
        packed = jnp.zeros((group, TILE), F32)
        for j in range(lanes):
            count = min(share - j * group, group)
            if count <= 0:
                continue
            part = rows_dt[
                shard * share + j * group : shard * share + j * group + count,
                j * TILE : (j + 1) * TILE,
            ]
            if count < group:
                part = jnp.concatenate([part, jnp.zeros((group - count, TILE), F32)], axis=0)
            packed = packed + part
        sums[-1][start : start + group] = packed
        sums[-1][start + group : start + unit] = small_ref[...]
    copy(0, planes - 1).start()

    for tick in range(levels + planes - 1):
        for plane in range(planes):
            k = tick - plane
            if not 0 <= k < levels:
                continue
            copy(k, plane).wait_recv()
            mine = half(k, plane, bits[k])
            sums[plane][mine] = sums[plane][mine] + gets[plane][k][...]
            if k + 1 < levels:
                copy(k + 1, plane).start()
    for plane in range(planes - 1):
        start = pl.multiple_of(offsets[levels] * share, 8)
        gbc_ref[:, plane * TILE : (plane + 1) * TILE] = sums[plane][pl.ds(start, share)]
    last = sums[-1][pl.ds(pl.multiple_of(offsets[levels] * unit, 8), unit)]
    for j in range(lanes):
        count = min(share - j * group, group)
        if count > 0:
            gdt_ref[j * group : j * group + count] = last[:count, j * heads : (j + 1) * heads]
    gbias_ref[...] = last[group : group + 1, :heads]
    grate_ref[...] = last[group + 1 : group + 2, :heads]
    gskip_ref[...] = last[group + 2 : group + 3, :heads]
    for plane in range(planes):
        for k in range(levels):
            copy(k, plane).wait_send()


def reduce_rows(devices, heads, layer_in, grad_proj, small):
    depth = layer_in.shape[1]
    wide = grad_proj.shape[1] - heads
    share, lanes, group = packing(depth, devices, heads)
    levels = devices.bit_length() - 1
    units = [share] * (wide // TILE) + [group + 8]
    scratch = [pltpu.VMEM((devices * unit, TILE), F32) for unit in units]
    for unit in units:
        scratch += [pltpu.VMEM(((devices >> (k + 1)) * unit, TILE), F32) for k in range(levels)]
    scratch.append(pltpu.SemaphoreType.DMA((2, levels, len(units))))
    shapes = [(share, wide), (share, heads), (1, heads), (1, heads), (1, heads)]
    return pl.pallas_call(
        functools.partial(reduce_kernel, devices, heads),
        out_shape=[jax.ShapeDtypeStruct(shape, F32) for shape in shapes],
        in_specs=[VMEM] * 3,
        out_specs=[VMEM] * 5,
        scratch_shapes=scratch,
        compiler_params=pltpu.CompilerParams(
            collective_id=1, has_side_effects=True, vmem_limit_bytes=VMEM_LIMIT
        ),
        name="reduce_rows",
    )(layer_in, grad_proj, small)


def call(kernel, shapes, name, *operands):
    return pl.pallas_call(
        kernel,
        out_shape=[jax.ShapeDtypeStruct(shape, dtype) for shape, dtype in shapes],
        in_specs=[VMEM] * len(operands),
        out_specs=[VMEM] * len(shapes),
        compiler_params=pltpu.CompilerParams(vmem_limit_bytes=VMEM_LIMIT),
        name=name,
    )(*operands)


def local(layer_in, ssm_in, weight_bc, weight_dt, bias_dt, log_rate, skip_gain, grad_out):
    tokens, depth = layer_in.shape
    heads = log_rate.shape[0]
    width = ssm_in.shape[1]
    state_dim = weight_bc.shape[1] // 2
    head_size = width // heads
    devices = lax.axis_size("seq")
    bias, rate, gain = bias_dt[None, :], log_rate[None, :], skip_gain[None, :]
    proj, raw, run, run_rows, states, total, scores, skip_sum, u, runx = call(
        before_kernel,
        [
            ((tokens, 2 * state_dim), BF16),
            ((tokens, heads), F32),
            ((tokens, heads), F32),
            ((heads, 1, tokens), F32),
            ((2, state_dim, width), F32),
            ((8, TILE), F32),
            ((tokens, tokens), F32),
            ((8, heads), F32),
            ((tokens, width), BF16),
            ((tokens, heads * TILE), F32),
        ],
        "before",
        layer_in, ssm_in, weight_bc, weight_dt, bias, rate, grad_out,
    )
    ends = scan_states(devices, heads, states, total)
    gu, rows, gscores = call(
        functools.partial(inner_kernel, head_size),
        [((tokens, width), F32), ((heads, 1, tokens), F32), ((tokens, tokens), F32)],
        "inner",
        u, grad_out, scores, runx, run_rows,
    )
    grad_ssm_in, grad_layer_in, grad_proj, small = call(
        after_kernel,
        [
            ((tokens, width), BF16),
            ((tokens, depth), BF16),
            ((tokens, 2 * state_dim + heads), BF16),
            ((8, TILE), F32),
        ],
        "after",
        ssm_in, grad_out, proj, raw, run, u, rate, gain, gu, rows, gscores, ends,
        weight_bc, weight_dt, skip_sum,
    )
    grad_bc, grad_dt, grad_bias, grad_rate, grad_skip = reduce_rows(
        devices, heads, layer_in, grad_proj, small
    )
    return (
        grad_ssm_in,
        grad_layer_in,
        grad_bc,
        grad_dt,
        grad_bias[0],
        grad_rate[0],
        grad_skip[0],
    )


def solution(mesh):
    rows = P(("groups", "seq"), None)
    in_specs = (rows, rows, P(), P(), P(), P(), P(), rows)
    out_specs = (rows, rows, rows, rows, P("groups"), P("groups"), P("groups"))
    return jax.shard_map(local, mesh=mesh, in_specs=in_specs, out_specs=out_specs, check_vma=False)
```

```python
import functools
import jax
import jax.numpy as jnp
from jax import lax
from jax.experimental import pallas as pl
from jax.experimental.pallas import tpu as pltpu
from jax.sharding import PartitionSpec as P

F32 = jnp.float32
BF16 = jnp.bfloat16
TILE = 128
CHUNKS = 4
VMEM_LIMIT = 60 * 1024 * 1024
VMEM = pl.BlockSpec(memory_space=pltpu.VMEM)


def mm(left, right):
    return lax.dot_general(left, right, (((1,), (0,)), ((), ())), preferred_element_type=F32)


def mm_nt(left, right):
    return lax.dot_general(left, right, (((1,), (1,)), ((), ())), preferred_element_type=F32)


def mm_tn(left, right):
    return lax.dot_general(left, right, (((0,), (0,)), ((), ())), preferred_element_type=F32)


def three_way(x):
    high = x.astype(BF16)
    rest = x - high.astype(F32)
    middle = rest.astype(BF16)
    return high, middle, (rest - middle.astype(F32)).astype(BF16)


def one_hot(heads, width, columns, first=0):
    row = lax.broadcasted_iota(jnp.int32, (heads, columns), 0)
    col = lax.broadcasted_iota(jnp.int32, (heads, columns), 1) + first
    inside = (col >= row * width) & (col < (row + 1) * width)
    return jnp.where(inside, 1.0, 0.0).astype(BF16)


def spread_heads(x, hot):
    parts = three_way(x)
    return mm(parts[0], hot) + mm(parts[1], hot) + mm(parts[2], hot)


def head_sum(x, hot):
    high = x.astype(BF16)
    low = (x - high.astype(F32)).astype(BF16)
    return mm_nt(high, hot) + mm_nt(low, hot)


def exact_mm(mask, x):
    parts = three_way(x)
    return mm(mask, parts[0]) + mm(mask, parts[1]) + mm(mask, parts[2])


def triangle(size, compare):
    row = lax.broadcasted_iota(jnp.int32, (size, size), 0)
    col = lax.broadcasted_iota(jnp.int32, (size, size), 1)
    return jnp.where(compare(row, col), 1.0, 0.0).astype(BF16)


def before_kernel(
    layer_ref, values_ref, wbc_ref, wdt_ref, bias_ref, rate_ref, grad_ref,
    proj_ref, raw_ref, run_ref, run_rows_ref, states_ref, total_ref, scores_ref, skip_ref,
    u_ref, runx_ref,
):
    tokens = layer_ref.shape[0]
    heads = bias_ref.shape[1]
    width = values_ref.shape[1]
    head_size = width // heads
    state_dim = wbc_ref.shape[1] // 2
    layer = layer_ref[...]
    proj = mm(layer, wbc_ref[...]).astype(BF16)
    proj_ref[...] = proj
    b_rows = proj[:, :state_dim]
    c_rows = proj[:, state_dim:]
    scores_ref[...] = mm_nt(b_rows, c_rows)
    raw = mm_nt(layer, wdt_ref[...]) + bias_ref[...]
    raw_ref[...] = raw
    step = jnp.maximum(raw, 0.0) + jnp.log1p(jnp.exp(-jnp.abs(raw)))
    decay = -jnp.exp(rate_ref[...]) * step
    run = exact_mm(triangle(tokens, lambda r, c: r >= c), decay)
    run_ref[...] = run
    run_rows = run.T
    for head in range(heads):
        run_rows_ref[head] = run_rows[head : head + 1]
    total = run[tokens - 1 :, :]
    total_ref[...] = jnp.zeros_like(total_ref)
    total_ref[:, :heads] = jnp.broadcast_to(total, (total_ref.shape[0], heads))
    hot = one_hot(heads, head_size, width)
    values = values_ref[...].astype(F32)
    grad = grad_ref[...].astype(F32)
    u_ref[...] = (spread_heads(step, hot) * values).astype(BF16)
    tail = spread_heads(jnp.exp(total - run) * step, hot)
    states_ref[0] = mm_tn(b_rows, (tail * values).astype(BF16))
    lead = spread_heads(jnp.exp(run), hot)
    states_ref[1] = mm_tn(c_rows, (lead * grad).astype(BF16))
    products = jnp.sum(values * grad, axis=0, keepdims=True)
    skip_ref[...] = head_sum(jnp.broadcast_to(products, (8, width)), hot)
    wide = one_hot(heads, TILE, heads * TILE)
    runx_ref[...] = spread_heads(run, wide)


def inner_pair(pair, u_ref, grad_ref, scores_ref, runx_ref, run_rows_ref,
               gu_ref, rows_ref, gscores_ref, head_size):
    tokens = u_ref.shape[0]
    blocks = tokens // TILE
    per = TILE // head_size
    cols = pl.ds(pl.multiple_of(pair * TILE, TILE), TILE)
    lane = lax.broadcasted_iota(jnp.int32, (TILE, TILE), 1)
    causal = lax.broadcasted_iota(jnp.int32, (TILE, TILE), 0) <= lane
    grads = [grad_ref[t * TILE : (t + 1) * TILE, cols] for t in range(blocks)]
    gus = [jnp.zeros((TILE, TILE), F32) for _ in range(blocks)]
    for sub in range(per):
        head = pair * per + sub
        keep = (lane >= sub * head_size) & (lane < (sub + 1) * head_size)
        hcols = pl.ds(pl.multiple_of(head * TILE, TILE), TILE)
        rows = [jnp.zeros((1, TILE), F32) for _ in range(blocks)]
        for s in range(blocks):
            srange = slice(s * TILE, (s + 1) * TILE)
            run_col = runx_ref[srange, hcols]
            u_head = jnp.where(keep, u_ref[srange, cols], jnp.zeros((), BF16))
            gu = jnp.zeros((TILE, TILE), F32)
            for t in range(s, blocks):
                trange = slice(t * TILE, (t + 1) * TILE)
                gap = run_rows_ref[head, :, trange] - run_col
                if s == t:
                    gap = jnp.where(causal, gap, -jnp.inf)
                factor = jnp.exp(gap)
                mixing = (factor * scores_ref[srange, trange]).astype(BF16)
                weight = mm_nt(u_head, grads[t])
                gscores_ref[srange, trange] += factor * weight
                rows[t] += jnp.sum(mixing.astype(F32) * weight, axis=0, keepdims=True)
                gu += mm(mixing, grads[t])
            gus[s] = jnp.where(keep, gu, gus[s])
        for t in range(blocks):
            rows_ref[head, :, t * TILE : (t + 1) * TILE] = rows[t]
    for s in range(blocks):
        gu_ref[s * TILE : (s + 1) * TILE, cols] = gus[s]


def scan_plan(devices, rows):
    levels = devices.bit_length() - 1
    sizes, halved = [rows], []
    for level in range(levels - 1):
        cut = sizes[-1] >= 16
        halved.append(cut)
        sizes.append(sizes[-1] // 2 if cut else sizes[-1])
    return levels, sizes, halved


def scan_kernel(devices, heads, states_ref, total_ref, u_ref, grad_ref, scores_ref, runx_ref,
                run_rows_ref, out_ref, gu_ref, rows_ref, gscores_ref, *refs):
    rows, width = states_ref.shape[1], states_ref.shape[2]
    head_size = width // heads
    levels, sizes, halved = scan_plan(devices, rows)
    top = levels - 1
    refs = list(refs)
    aggs = [states_ref] + [refs.pop(0) for _ in range(top)]
    gets = [refs.pop(0) for _ in range(top)]
    outs = [out_ref] + [refs.pop(0) for _ in range(top)]
    sends = [refs.pop(0) if halved[k] else None for k in range(top)]
    downs = [refs.pop(0) if halved[k] else None for k in range(top)]
    top_get, tots, tot_gets, decays, up_sems, down_sems, tot_sems = refs
    me = lax.axis_index("seq")
    bits = [lax.rem(me // (1 << k), 2) for k in range(levels)]
    partners = [me + (1 - 2 * bits[k]) * (1 << k) for k in range(levels)]
    barrier = pltpu.get_barrier_semaphore()
    for k in range(levels):
        pl.semaphore_signal(
            barrier, inc=1, device_id={"seq": partners[k]}, device_id_type=pl.DeviceIdType.MESH
        )
    pl.semaphore_wait(barrier, levels)
    span = width // CHUNKS

    def copy(source, target, send, receive, k):
        return pltpu.make_async_remote_copy(
            src_ref=source, dst_ref=target, send_sem=send, recv_sem=receive,
            device_id={"seq": partners[k]}, device_id_type=pl.DeviceIdType.MESH,
        )

    def half_at(k, which):
        size = sizes[k + 1]
        return pl.ds(pl.multiple_of(which * size, 8), size)

    def up_copy(k, c):
        cols = slice(c * span, (c + 1) * span)
        if k == top:
            source, target = aggs[k].at[bits[k], :, cols], top_get.at[:, cols]
        elif halved[k]:
            source, target = aggs[k].at[:, half_at(k, 1 - bits[k]), cols], gets[k].at[:, :, cols]
        else:
            source, target = aggs[k].at[:, :, cols], gets[k].at[:, :, cols]
        return copy(source, target, up_sems.at[0, k, c], up_sems.at[1, k, c], k)

    def down_copy(k, c):
        cols = slice(c * span, (c + 1) * span)
        return copy(sends[k].at[:, :, cols], downs[k].at[:, :, cols],
                    down_sems.at[0, k, c], down_sems.at[1, k, c], k)

    def tot_copy(k):
        return copy(tots.at[k], tot_gets.at[k], tot_sems.at[0, k], tot_sems.at[1, k], k)

    def tot_done(k):
        tot_copy(k).wait_recv()
        mine, other = tots[k], tot_gets[k]
        tots[k + 1] = mine + other
        left = jnp.where(bits[k] == 0, mine, other)
        right = jnp.where(bits[k] == 0, other, mine)
        hot = one_hot(TILE, head_size, width)
        decays[k, 0] = jnp.exp(spread_heads(left, hot))
        decays[k, 1] = jnp.exp(spread_heads(right, hot))

    def own(k, cols, part):
        if halved[k]:
            return aggs[k][part, half_at(k, bits[k]), cols]
        return aggs[k][part, :, cols]

    def finish_up(k, c):
        cols = slice(c * span, (c + 1) * span)
        up_copy(k, c).wait_recv()
        if c == 0:
            tot_done(k)
            if k + 1 < top:
                tot_copy(k + 1).start()
        first = bits[k] == 0
        s_mine, g_mine = own(k, cols, 0), own(k, cols, 1)
        s_got, g_got = gets[k][0, :, cols], gets[k][1, :, cols]
        s_left, s_right = jnp.where(first, s_mine, s_got), jnp.where(first, s_got, s_mine)
        g_left, g_right = jnp.where(first, g_mine, g_got), jnp.where(first, g_got, g_mine)
        aggs[k + 1][0, :, cols] = decays[k, 1, 0:1, cols] * s_left + s_right
        aggs[k + 1][1, :, cols] = g_left + decays[k, 0, 0:1, cols] * g_right
        up_copy(k + 1, c).start()

    def finish_top(c):
        cols = slice(c * span, (c + 1) * span)
        up_copy(top, c).wait_recv()
        got = top_get[:, cols]
        zero = jnp.zeros_like(got)
        outs[top][0, :, cols] = jnp.where(bits[top] == 1, got, zero)
        outs[top][1, :, cols] = jnp.where(bits[top] == 1, zero, got)
        if top > 0:
            step_down(top - 1, c)

    def step_down(k, c):
        cols = slice(c * span, (c + 1) * span)
        first = bits[k] == 0
        inc, outg = outs[k + 1][0, :, cols], outs[k + 1][1, :, cols]
        s_left = jnp.where(first, own(k, cols, 0), gets[k][0, :, cols])
        g_right = jnp.where(first, gets[k][1, :, cols], own(k, cols, 1))
        right_in = decays[k, 0, 0:1, cols] * inc + s_left
        left_out = decays[k, 1, 0:1, cols] * outg + g_right
        if halved[k]:
            sends[k][0, :, cols] = jnp.where(first, right_in, inc)
            sends[k][1, :, cols] = jnp.where(first, outg, left_out)
            down_copy(k, c).start()
            mine = half_at(k, bits[k])
        else:
            mine = slice(None)
        outs[k][0, mine, cols] = jnp.where(first, inc, right_in)
        outs[k][1, mine, cols] = jnp.where(first, left_out, outg)

    def finish_down(k, c):
        cols = slice(c * span, (c + 1) * span)
        if halved[k]:
            down_copy(k, c).wait_recv()
            outs[k][:, half_at(k, 1 - bits[k]), cols] = downs[k][:, :, cols]
        if k > 0:
            step_down(k - 1, c)

    tots[0] = total_ref[...]
    if top > 0:
        tot_copy(0).start()
    for c in range(CHUNKS):
        up_copy(0, c).start()
    stages = [functools.partial(finish_up, k) for k in range(top)]
    stages.append(finish_top)
    stages += [functools.partial(finish_down, k) for k in reversed(range(top))]
    gscores_ref[...] = jnp.zeros_like(gscores_ref)

    def body(pair, _):
        inner_pair(pair, u_ref, grad_ref, scores_ref, runx_ref, run_rows_ref,
                   gu_ref, rows_ref, gscores_ref, head_size)
        return 0

    pairs = width // TILE
    ticks = len(stages) + CHUNKS - 1
    for tick in range(ticks):
        lax.fori_loop(tick * pairs // ticks, (tick + 1) * pairs // ticks, body, 0)
        for c in range(CHUNKS):
            if 0 <= tick - c < len(stages):
                stages[tick - c](c)
    for k in range(top):
        tot_copy(k).wait_send()
    for c in range(CHUNKS):
        for k in range(levels):
            up_copy(k, c).wait_send()
        for k in range(top):
            if halved[k]:
                down_copy(k, c).wait_send()


def scan_states(devices, heads, states, total, u, grad, scores, runx, run_rows):
    rows, width = states.shape[1], states.shape[2]
    levels, sizes, halved = scan_plan(devices, rows)
    top = levels - 1
    scratch = [pltpu.VMEM((2, sizes[k + 1], width), F32) for k in range(top)]
    scratch += [pltpu.VMEM((2, sizes[k + 1], width), F32) for k in range(top)]
    scratch += [pltpu.VMEM((2, sizes[k + 1], width), F32) for k in range(top)]
    for _ in range(2):
        scratch += [pltpu.VMEM((2, sizes[k + 1], width), F32) for k in range(top) if halved[k]]
    scratch += [
        pltpu.VMEM((sizes[top], width), F32),
        pltpu.VMEM((levels + 1, 8, TILE), F32),
        pltpu.VMEM((levels, 8, TILE), F32),
        pltpu.VMEM((levels, 2, 8, width), F32),
        pltpu.SemaphoreType.DMA((2, levels, CHUNKS)),
        pltpu.SemaphoreType.DMA((2, levels, CHUNKS)),
        pltpu.SemaphoreType.DMA((2, levels)),
    ]
    return pl.pallas_call(
        functools.partial(scan_kernel, devices, heads),
        out_shape=[
            jax.ShapeDtypeStruct(shape, F32)
            for shape in (states.shape, u.shape, run_rows.shape, scores.shape)
        ],
        in_specs=[VMEM] * 7,
        out_specs=[VMEM] * 4,
        scratch_shapes=scratch,
        compiler_params=pltpu.CompilerParams(
            collective_id=0, has_side_effects=True, vmem_limit_bytes=VMEM_LIMIT
        ),
        name="scan_states",
    )(states, total, u, grad, scores, runx, run_rows)


def after_kernel(
    values_ref, grad_ref, proj_ref, raw_ref, run_ref, u_ref, rate_ref, skip_ref,
    gu_ref, rows_ref, gscores_ref, ends_ref, wbc_ref, wdt_ref, skip_sum_ref,
    gvalues_ref, glayer_ref, gproj_ref, small_ref,
):
    tokens, heads = raw_ref.shape
    width = values_ref.shape[1]
    head_size = width // heads
    state_dim = proj_ref.shape[1] // 2
    hot = one_hot(heads, head_size, width)
    raw, run = raw_ref[...], run_ref[...]
    rate = jnp.exp(rate_ref[...])
    step = jnp.maximum(raw, 0.0) + jnp.log1p(jnp.exp(-jnp.abs(raw)))
    total = run[tokens - 1 :, :]
    b_rows = proj_ref[:, :state_dim]
    c_rows = proj_ref[:, state_dim:]
    incoming, outgoing = ends_ref[0], ends_ref[1]
    inc_b, out_b = incoming.astype(BF16), outgoing.astype(BF16)
    values = values_ref[...].astype(F32)
    grad = grad_ref[...].astype(F32)
    step_wide = spread_heads(step, hot)
    lead_grad = spread_heads(jnp.exp(run), hot) * grad
    lead_b = lead_grad.astype(BF16)
    reads = head_sum(lead_grad * mm(c_rows, inc_b), hot)
    gscores = gscores_ref[...].astype(BF16)
    grad_c = mm_nt(lead_b, inc_b) + mm_tn(gscores, b_rows)
    tail_wide = spread_heads(jnp.exp(total - run), hot)
    back = tail_wide * mm(b_rows, out_b)
    grad_b = mm_nt((tail_wide * step_wide * values).astype(BF16), out_b) + mm(gscores, c_rows)
    gu = gu_ref[...]
    inner_cols = head_sum(u_ref[...].astype(F32) * gu, hot)
    back_sum = head_sum(values * back, hot)
    gu = gu + back
    gvalues_ref[...] = (step_wide * gu + spread_heads(skip_ref[...], hot) * grad).astype(BF16)
    grad_step = head_sum(values * gu, hot)
    cross = jnp.sum(incoming * outgoing, axis=0, keepdims=True)
    cross = head_sum(jnp.broadcast_to(cross, (8, width)), hot)[0:1]
    upper = triangle(tokens, lambda r, c: r <= c)
    lower = triangle(tokens, lambda r, c: r > c)
    inner = rows_ref[:, 0, :].T + reads - inner_cols
    grad_decay = exact_mm(upper, inner) + exact_mm(lower, step * back_sum) + jnp.exp(total) * cross
    sigmoid = 1.0 / (1.0 + jnp.exp(-raw))
    grad_raw = (grad_step - rate * grad_decay) * sigmoid
    gproj_ref[:, :state_dim] = grad_b.astype(BF16)
    gproj_ref[:, state_dim : 2 * state_dim] = grad_c.astype(BF16)
    gproj_ref[:, 2 * state_dim :] = grad_raw.astype(BF16)
    small_ref[...] = jnp.zeros_like(small_ref)
    small_ref[0:1, :heads] = jnp.sum(grad_raw, axis=0, keepdims=True)
    small_ref[1:2, :heads] = -rate * jnp.sum(grad_decay * step, axis=0, keepdims=True)
    small_ref[2:3, :heads] = skip_sum_ref[0:1]
    glayer_ref[...] = (
        mm_nt(gproj_ref[:, : 2 * state_dim], wbc_ref[...])
        + mm(grad_raw.astype(BF16), wdt_ref[...])
    ).astype(BF16)


def packing(depth, devices, heads):
    share = depth // devices
    lanes = TILE // heads
    group = -(-share // (8 * lanes)) * 8
    return share, lanes, group


def reduce_kernel(devices, heads, layer_ref, gproj_ref, small_ref,
                  gbc_ref, gdt_ref, gbias_ref, grate_ref, gskip_ref, *refs):
    depth = layer_ref.shape[1]
    share, lanes, group = packing(depth, devices, heads)
    levels = devices.bit_length() - 1
    wide = gbc_ref.shape[1]
    planes = wide // TILE + 1
    refs = list(refs)
    sems = refs.pop()
    sums = [refs.pop(0) for _ in range(planes)]
    gets = [[refs.pop(0) for _ in range(levels)] for _ in range(planes)]
    units = [share] * (planes - 1) + [group + 8]
    me = lax.axis_index("seq")
    bits = [lax.rem(me // (1 << k), 2) for k in range(levels)]
    partners = [me + (1 - 2 * bits[k]) * (1 << k) for k in range(levels)]
    offsets = [0]
    for k in range(levels):
        offsets.append(offsets[k] + bits[k] * (devices >> (k + 1)))
    barrier = pltpu.get_barrier_semaphore()
    for k in range(levels):
        pl.semaphore_signal(
            barrier, inc=1, device_id={"seq": partners[k]}, device_id_type=pl.DeviceIdType.MESH
        )
    pl.semaphore_wait(barrier, levels)
    places = [
        sum(((shard >> k) & 1) * (devices >> (k + 1)) for k in range(levels))
        for shard in range(devices)
    ]

    def half(k, plane, which):
        size = (devices >> (k + 1)) * units[plane]
        start = (offsets[k] + which * (devices >> (k + 1))) * units[plane]
        return pl.ds(pl.multiple_of(start, 8), size)

    def copy(k, plane):
        return pltpu.make_async_remote_copy(
            src_ref=sums[plane].at[half(k, plane, 1 - bits[k])],
            dst_ref=gets[plane][k],
            send_sem=sems.at[0, k, plane],
            recv_sem=sems.at[1, k, plane],
            device_id={"seq": partners[k]},
            device_id_type=pl.DeviceIdType.MESH,
        )

    layer = layer_ref[...]
    rows_bc = mm_tn(layer, gproj_ref[:, :wide])
    for plane in range(planes - 1):
        for shard in range(devices):
            sums[plane][places[shard] * share : (places[shard] + 1) * share] = rows_bc[
                shard * share : (shard + 1) * share, plane * TILE : (plane + 1) * TILE
            ]
        copy(0, plane).start()
    row = lax.broadcasted_iota(jnp.int32, (heads, lanes * TILE), 0)
    col = lax.broadcasted_iota(jnp.int32, (heads, lanes * TILE), 1)
    shift = jnp.zeros(row.shape, F32)
    for j in range(lanes):
        shift = jnp.where(col == row + j * (TILE + heads), 1.0, shift)
    moved = mm(gproj_ref[:, wide:], shift.astype(BF16)).astype(BF16)
    rows_dt = mm_tn(layer, moved)
    unit = group + 8
    for shard in range(devices):
        start = places[shard] * unit
        packed = jnp.zeros((group, TILE), F32)
        for j in range(lanes):
            count = min(share - j * group, group)
            if count <= 0:
                continue
            part = rows_dt[
                shard * share + j * group : shard * share + j * group + count,
                j * TILE : (j + 1) * TILE,
            ]
            if count < group:
                part = jnp.concatenate([part, jnp.zeros((group - count, TILE), F32)], axis=0)
            packed = packed + part
        sums[-1][start : start + group] = packed
        sums[-1][start + group : start + unit] = small_ref[...]
    copy(0, planes - 1).start()

    for tick in range(levels + planes - 1):
        for plane in range(planes):
            k = tick - plane
            if not 0 <= k < levels:
                continue
            copy(k, plane).wait_recv()
            mine = half(k, plane, bits[k])
            sums[plane][mine] = sums[plane][mine] + gets[plane][k][...]
            if k + 1 < levels:
                copy(k + 1, plane).start()
    for plane in range(planes - 1):
        start = pl.multiple_of(offsets[levels] * share, 8)
        gbc_ref[:, plane * TILE : (plane + 1) * TILE] = sums[plane][pl.ds(start, share)]
    last = sums[-1][pl.ds(pl.multiple_of(offsets[levels] * unit, 8), unit)]
    for j in range(lanes):
        count = min(share - j * group, group)
        if count > 0:
            gdt_ref[j * group : j * group + count] = last[:count, j * heads : (j + 1) * heads]
    gbias_ref[...] = last[group : group + 1, :heads]
    grate_ref[...] = last[group + 1 : group + 2, :heads]
    gskip_ref[...] = last[group + 2 : group + 3, :heads]
    for plane in range(planes):
        for k in range(levels):
            copy(k, plane).wait_send()


def reduce_rows(devices, heads, layer_in, grad_proj, small):
    depth = layer_in.shape[1]
    wide = grad_proj.shape[1] - heads
    share, lanes, group = packing(depth, devices, heads)
    levels = devices.bit_length() - 1
    units = [share] * (wide // TILE) + [group + 8]
    scratch = [pltpu.VMEM((devices * unit, TILE), F32) for unit in units]
    for unit in units:
        scratch += [pltpu.VMEM(((devices >> (k + 1)) * unit, TILE), F32) for k in range(levels)]
    scratch.append(pltpu.SemaphoreType.DMA((2, levels, len(units))))
    shapes = [(share, wide), (share, heads), (1, heads), (1, heads), (1, heads)]
    return pl.pallas_call(
        functools.partial(reduce_kernel, devices, heads),
        out_shape=[jax.ShapeDtypeStruct(shape, F32) for shape in shapes],
        in_specs=[VMEM] * 3,
        out_specs=[VMEM] * 5,
        scratch_shapes=scratch,
        compiler_params=pltpu.CompilerParams(
            collective_id=1, has_side_effects=True, vmem_limit_bytes=VMEM_LIMIT
        ),
        name="reduce_rows",
    )(layer_in, grad_proj, small)


def call(kernel, shapes, name, *operands):
    return pl.pallas_call(
        kernel,
        out_shape=[jax.ShapeDtypeStruct(shape, dtype) for shape, dtype in shapes],
        in_specs=[VMEM] * len(operands),
        out_specs=[VMEM] * len(shapes),
        compiler_params=pltpu.CompilerParams(vmem_limit_bytes=VMEM_LIMIT),
        name=name,
    )(*operands)


def local(layer_in, ssm_in, weight_bc, weight_dt, bias_dt, log_rate, skip_gain, grad_out):
    tokens, depth = layer_in.shape
    heads = log_rate.shape[0]
    width = ssm_in.shape[1]
    state_dim = weight_bc.shape[1] // 2
    head_size = width // heads
    devices = lax.axis_size("seq")
    narrow = weight_dt.T
    bias, rate, gain = bias_dt[None, :], log_rate[None, :], skip_gain[None, :]
    proj, raw, run, run_rows, states, total, scores, skip_sum, u, runx = call(
        before_kernel,
        [
            ((tokens, 2 * state_dim), BF16),
            ((tokens, heads), F32),
            ((tokens, heads), F32),
            ((heads, 1, tokens), F32),
            ((2, state_dim, width), F32),
            ((8, TILE), F32),
            ((tokens, tokens), F32),
            ((8, heads), F32),
            ((tokens, width), BF16),
            ((tokens, heads * TILE), F32),
        ],
        "before",
        layer_in, ssm_in, weight_bc, narrow, bias, rate, grad_out,
    )
    ends, gu, rows, gscores = scan_states(
        devices, heads, states, total, u, grad_out, scores, runx, run_rows
    )
    grad_ssm_in, grad_layer_in, grad_proj, small = call(
        after_kernel,
        [
            ((tokens, width), BF16),
            ((tokens, depth), BF16),
            ((tokens, 2 * state_dim + heads), BF16),
            ((8, TILE), F32),
        ],
        "after",
        ssm_in, grad_out, proj, raw, run, u, rate, gain, gu, rows, gscores, ends,
        weight_bc, narrow, skip_sum,
    )
    grad_bc, grad_dt, grad_bias, grad_rate, grad_skip = reduce_rows(
        devices, heads, layer_in, grad_proj, small
    )
    return (
        grad_ssm_in,
        grad_layer_in,
        grad_bc,
        grad_dt,
        grad_bias[0],
        grad_rate[0],
        grad_skip[0],
    )


def solution(mesh):
    rows = P(("groups", "seq"), None)
    in_specs = (rows, rows, P(), P(), P(), P(), P(), rows)
    out_specs = (rows, rows, rows, rows, P("groups"), P("groups"), P("groups"))
    return jax.shard_map(local, mesh=mesh, in_specs=in_specs, out_specs=out_specs, check_vma=False)
```
